32 devices in a mesh: groups: 2 (over x), blk: 8 (over z, y), split: 2 (over core).
Axes of the slice: x: 2, y: 2, z: 4, core: 2. Of those that a mesh axis runs over, the one named last changes fastest.
Arguments:
- embeddings: bfloat16 [32768, 768], P(('groups', 'blk', 'split')), parts along dimension 0, may hold values from -6 to 6
- cluster_of: int32 [32768], P(('groups', 'blk', 'split')), parts along dimension 0, may hold values from 0 to 15, as said below
- target_pos: int32 [32768], P(('groups', 'blk', 'split')), parts along dimension 0, may hold values from 0 to 16383, as said below
Outputs:
- best: float32 [32768], P(('groups', 'blk', 'split')), parts along dimension 0
The draws below stay inside these ranges and needn't reach their ends.
There are 2 independent parts, one for each index of `groups`. The reference program is written for one: setup_inputs(seed, part) draws one part's arguments, and reference() takes and returns one part's arrays. A program takes and returns all parts, laid end to end along the dimension named above; each array names one. Nothing has to cross between parts.
Inputs may be any that keep to these rules, and one draw needn't show every extreme that they name: `cluster_of`: ordering the members by target_pos lists cluster 0 first, then cluster 1 and so on, each cluster's members contiguous; every cluster has 2 to 4096 members and one has exactly 4096. `target_pos`: A permutation of the rows. For every aligned block of 1024 positions, each device's 1024 data-order rows hold exactly 64 of its positions.
All inputs are finite; a program needn't handle non-finite values.
Results may differ from the reference program's by a relative error of at most 0.0025.
Values may be sent and summed in bfloat16 or wider, within the bound.
A program may use at most 64 MiB of HBM per device.

```python
import jax
import jax.numpy as jnp
from jax import lax

D = 768
ROWS_DEV = 1024
DEVS_PART = 16
ROWS = 16384
CLUSTERS = 16
MOST = 4096


def layout_draw(key):
    key = jax.random.fold_in(key, 7)
    key_big, key_weights, key_blocks, key_shuffle = jax.random.split(key, 4)
    count = DEVS_PART
    rows = ROWS_DEV
    total = ROWS
    index = jnp.arange(CLUSTERS, dtype=jnp.int32)
    big = jax.random.randint(key_big, (), 0, CLUSTERS)
    weights = jax.random.randint(key_weights, (CLUSTERS,), 4, 8)
    others = index != big
    weights = jnp.where(others, weights, 0)
    spare = total - MOST - 2 * (CLUSTERS - 1)
    share = weights * spare // jnp.sum(weights)
    leftover = spare - jnp.sum(share)
    ranks = jnp.cumsum(others.astype(jnp.int32)) - 1
    extra = ((ranks < leftover) & others).astype(jnp.int32)
    sizes = jnp.where(others, 2 + share + extra, MOST).astype(jnp.int32)
    ends = jnp.cumsum(sizes)
    position = jnp.arange(total, dtype=jnp.int32)
    sorted_ids = jnp.sum((position[:, None] >= ends[None, :]).astype(jnp.int32), axis=1).astype(jnp.int32)
    perms = jax.vmap(lambda k: jax.random.permutation(k, rows))(jax.random.split(key_blocks, count))
    blocks = (jnp.arange(count, dtype=jnp.int32)[:, None] * rows + perms.astype(jnp.int32)).reshape(count, count, rows // count)
    by_source = jnp.transpose(blocks, (1, 0, 2)).reshape(count, rows)
    shuffle = jax.vmap(lambda k: jax.random.permutation(k, rows))(jax.random.split(key_shuffle, count))
    by_source = jnp.take_along_axis(by_source, shuffle.astype(jnp.int32), axis=1)
    target = by_source.reshape(total).astype(jnp.int32)
    return (sorted_ids[target], target)


def draw_cluster_of(key, part):
    return layout_draw(key)[0]


def draw_target_pos(key, part):
    return layout_draw(key)[1]


def block_scale(key, extent, shards, least, high):
    gain = 1.0
    for dim, parts in shards:
        steps = jax.random.uniform(jax.random.fold_in(jax.random.fold_in(key, 6), dim), (parts,), jnp.float32, least / len(shards), high / len(shards))
        gain = gain * jnp.repeat(jnp.exp(steps), extent[dim] // parts).reshape((-1,) + (1,) * (len(extent) - 1 - dim))
    return gain


def normal_values(key, dims, width, bound, cuts=(), held_as=jnp.bfloat16):
    loudness = block_scale(key, dims, cuts, -0.22, 0.18) if cuts else 1.0
    array = jax.random.normal(key, dims, jnp.float32) * width * loudness
    return jnp.minimum(jnp.maximum(array, -bound), bound).astype(held_as)


def setup_inputs(seed: int = 0, part: int = 0) -> dict:
    arg_keys = jax.random.split(jax.random.key(seed), 4)
    part_keys = jax.random.split(jax.random.fold_in(arg_keys[3], part), 4)
    embeddings = normal_values(part_keys[0], (ROWS, D), 1.0, 6.0, ((0, 16),))
    cluster_of = draw_cluster_of(jax.random.fold_in(jax.random.fold_in(arg_keys[3], part), 71), part)
    target_pos = draw_target_pos(jax.random.fold_in(jax.random.fold_in(arg_keys[3], part), 71), part)
    return {"embeddings": embeddings, "cluster_of": cluster_of, "target_pos": target_pos}


def reference(embeddings, cluster_of, target_pos):
    values = embeddings.astype(jnp.float32)
    unit = (values * lax.rsqrt(lax.optimization_barrier(jnp.sum(values * values, axis=1, keepdims=True)) + 1e-06)).astype(jnp.bfloat16)
    sorted_unit = jnp.zeros((ROWS, D), jnp.bfloat16).at[target_pos].set(unit)
    sorted_ids = jnp.zeros((ROWS,), jnp.int32).at[target_pos].set(cluster_of)
    margin = MOST
    span = ROWS_DEV + 2 * margin
    pad_unit = jnp.concatenate([jnp.zeros((margin, D), jnp.bfloat16), sorted_unit, jnp.zeros((margin, D), jnp.bfloat16)], axis=0)
    pad_ids = jnp.concatenate([jnp.full((margin,), -1, jnp.int32), sorted_ids, jnp.full((margin,), -1, jnp.int32)], axis=0)

    def one_block(block):
        start = (block * ROWS_DEV).astype(jnp.int32)
        rows = lax.dynamic_slice_in_dim(sorted_unit, start, ROWS_DEV, 0)
        row_ids = lax.dynamic_slice_in_dim(sorted_ids, start, ROWS_DEV, 0)
        window = lax.dynamic_slice_in_dim(pad_unit, start, span, 0)
        window_ids = lax.dynamic_slice_in_dim(pad_ids, start, span, 0)
        sims = jnp.dot(rows, window.T, preferred_element_type=jnp.float32)
        row_pos = start + jnp.arange(ROWS_DEV, dtype=jnp.int32)
        window_pos = start - margin + jnp.arange(span, dtype=jnp.int32)
        keep = (row_ids[:, None] == window_ids[None, :]) & (row_pos[:, None] != window_pos[None, :])
        return lax.optimization_barrier(jnp.max(jnp.where(keep, sims, -4.0), axis=1))
    best_sorted = lax.map(one_block, jnp.arange(ROWS // ROWS_DEV, dtype=jnp.int32)).reshape(ROWS)
    return best_sorted[target_pos]
```

```python
import functools

import jax
import jax.numpy as jnp
from jax import lax
from jax.experimental import pallas as pl
from jax.experimental.pallas import tpu as pltpu
from jax.sharding import PartitionSpec as P

MOST = 4096
FILL = -4.0
MESH = pl.DeviceIdType.MESH
F32 = jnp.float32
BF16 = jnp.bfloat16


def nt(a, b):
    return lax.dot_general(a, b, (((1,), (1,)), ((), ())), preferred_element_type=F32)


def pack_kernel(n, emb, cl, tp, packed, idm, key_ref):
    rows, width = emb.shape
    piece = rows // n
    nq, cr = n // 4, 2 * piece
    shift = rows.bit_length() - 1
    x = emb[...].astype(F32)
    unit = (x * lax.rsqrt(jnp.sum(x * x, axis=1, keepdims=True) + 1e-06)).astype(BF16)
    dest = lax.shift_right_logical(tp[...], shift)
    hit = lax.broadcasted_iota(jnp.int32, (n, rows), 0) == dest
    hot = jnp.where(hit, 1.0, 0.0)
    i0 = lax.broadcasted_iota(jnp.int32, (rows, rows), 0)
    i1 = lax.broadcasted_iota(jnp.int32, (rows, rows), 1)
    before = jnp.where(i0 < i1, 1.0, 0.0).astype(BF16)
    counts = jnp.dot(hot.astype(BF16), before, preferred_element_type=F32)
    rank = jnp.sum(hot * counts, axis=0, keepdims=True).astype(jnp.int32)
    key = dest * piece + rank
    key_ref[...] = key
    perm = jnp.where(i0 == key, 1.0, 0.0).astype(BF16)
    zero = jnp.zeros((cr, width), BF16)
    packed[pl.ds(0, cr), :] = zero
    packed[pl.ds(cr, rows), :] = jnp.dot(perm, unit, preferred_element_type=F32).astype(BF16)
    packed[pl.ds(cr + rows, cr), :] = zero
    labels = jnp.broadcast_to(cl[...].astype(F32), (8, rows)).astype(BF16)
    ids = nt(labels, perm).astype(jnp.int32)[0:1]
    none = jnp.full((1, cr), -1, jnp.int32)
    padded = jnp.concatenate([none, ids, none], axis=1)
    for q in range(nq):
        idm[q, 0:1, :] = padded[:, 2 * cr * q : 2 * cr * (q + 1)]
        idm[q, 1:2, :] = padded[:, 2 * cr * (q + 1) : 2 * cr * (q + 2)]
        idm[q, 2:3, :] = ids[:, 2 * cr * q : 2 * cr * (q + 1)]
        idm[q, 3:8, :] = jnp.zeros((5, 2 * cr), jnp.int32)


def pick(table, hot):
    hi = table.astype(BF16)
    rest = table - hi.astype(F32)
    mid = rest.astype(BF16)
    low = (rest - mid.astype(F32)).astype(BF16)
    out = jnp.dot(hi, hot, preferred_element_type=F32)
    out += jnp.dot(mid, hot, preferred_element_type=F32)
    return out + jnp.dot(low, hot, preferred_element_type=F32)


def main_kernel(
    n, packed, idm, key_ref, out_ref,
    A, Q, IDS, MSG, MSGR, racc, cacc, colid, qid,
    init_s, recv, relay_s, y_s, y_r, c_s, c_r, d_s, d_r, loc, self_sem, ids_s, ids_r, msg_s, msg_r,
):
    nq = n // 4
    cr2 = packed.shape[1]
    cr = cr2 // 2
    rows = nq * cr2
    blk, split = lax.axis_index("blk"), lax.axis_index("split")
    me = blk * 2 + split
    q = blk // 2
    r = lax.rem(blk, 2) * 2 + split

    def dev(index):
        return {"blk": index // 2, "split": lax.rem(index, 2)}

    core = 4 * q + lax.rem(blk, 2) * 2 + (1 - split)
    across = 4 * q + lax.rem(r + 2, 4)
    rc = lax.rem(blk, 2) * 2 + (1 - split)
    ry = lax.rem(r + 2, 4)
    rd = lax.rem(rc + 2, 4)

    barrier = pltpu.get_barrier_semaphore()

    @pl.loop(1, n)
    def _(o):
        pl.semaphore_signal(
            barrier, inc=1, device_id=dev(lax.rem(me + o, n)), device_id_type=MESH
        )

    pl.semaphore_wait(barrier, n - 1)

    def remote(src, dst, s_sem, r_sem, index):
        return pltpu.make_async_remote_copy(
            src_ref=src, dst_ref=dst, send_sem=s_sem, recv_sem=r_sem,
            device_id=dev(index), device_id_type=MESH,
        )

    def ids_copy(o):
        to = lax.rem(me + o, n)
        return remote(idm.at[to // 4], IDS.at[me], ids_s.at[o], ids_r.at[me], to)

    def ids_in(o):
        frm = lax.rem(me + o, n)
        return remote(idm.at[0], IDS.at[frm], ids_s.at[o], ids_r.at[frm], frm)

    @pl.loop(1, n)
    def _(o):
        ids_copy(o).start()

    EDGE = {0: pl.ds(cr, cr), nq: pl.ds(0, cr)}

    def init(g):
        if g == 0:
            return q != 0, remote(
                packed.at[0, EDGE[0]], A.at[0, q, EDGE[0]], init_s.at[g], recv.at[0, q], r
            )
        if g == nq:
            return q != nq - 1, remote(
                packed.at[nq, EDGE[nq]], A.at[1, q, EDGE[nq]], init_s.at[g], recv.at[1, q],
                4 * (nq - 1) + r,
            )
        low = jnp.logical_or(q < g - 1, q == g)
        target = jnp.where(low, g - 1, g)
        side = g - target
        return None, remote(
            packed.at[g], A.at[side, q], init_s.at[g], recv.at[side, q], 4 * target + r
        )

    def when(cond, do):
        if cond is None:
            do()
        else:
            pl.when(cond)(do)

    for g in range(nq + 1):
        cond, copy = init(g)
        when(cond, copy.start)

    selfs = [pltpu.make_async_copy(packed.at[q + k], A.at[k, q], self_sem.at[k]) for k in (0, 1)]
    for copy in selfs:
        copy.start()

    @pl.loop(1, n)
    def _(o):
        ids_in(o).wait_recv()

    IDS[me] = idm[q]

    half = (pl.ds(cr, cr), pl.ds(0, cr))
    home = (pl.ds(0, cr), pl.ds(cr, cr))

    def parts(k, s):
        mine = A.at[k, s, half[k]]
        y = remote(mine, Q.at[r, s, home[k]], y_s.at[k, s], y_r.at[k, s], across)
        c = remote(mine, Q.at[r, s, home[k]], c_s.at[k, s], c_r.at[k, s], core)
        own = pltpu.make_async_copy(mine, Q.at[r, s, home[k]], loc.at[k, s])
        return y, c, own

    def forward(k, s):
        for copy in parts(k, s):
            copy.start()

    def y_in(k, s):
        return remote(A.at[k, s, half[k]], Q.at[ry, s, home[k]], y_s.at[k, s], y_r.at[k, s], across)

    def diag(k, s):
        there = Q.at[ry, s, home[k]]
        return remote(there, there, d_s.at[k, s], d_r.at[k, s], core)

    def diag_forward(k, s):
        y_in(k, s).wait_recv()
        diag(k, s).start()

    def c_in(k, s):
        return remote(A.at[k, s, half[k]], Q.at[rc, s, home[k]], c_s.at[k, s], c_r.at[k, s], core)

    def d_in(k, s):
        there = Q.at[rd, s, home[k]]
        return remote(there, there, d_s.at[k, s], d_r.at[k, s], core)

    def arrived(k, s, part=None):
        dst = A.at[k, s] if part is None else A.at[k, s, part]
        src = packed.at[0] if part is None else packed.at[0, part]
        remote(src, dst, relay_s.at[k, s], recv.at[k, s], me).wait_recv()

    def relay(k, s):
        to = me + 4 if k == 1 else me - 4
        return remote(A.at[k, s], A.at[1 - k, s], relay_s.at[k, s], recv.at[1 - k, s], to)

    last = {0: q == 0, 1: q == nq - 1}

    def first_stop(k, s):
        @pl.when(last[k])
        def _():
            arrived(k, s, half[k])

        @pl.when(jnp.logical_not(last[k]))
        def _():
            arrived(k, s)
            relay(k, s).start()

        forward(k, s)

    def second_stop(k, s):
        arrived(k, s)
        forward(k, s)

    def source(kind, k, d):
        below = (kind == "first") == (k == 1)
        s = q - d if below else q + d
        return s, (s >= 0 if below else s < nq)

    items = []
    order = [("first", 1), ("second", 1)]
    order += [("first", d) for d in range(2, nq)] + [("second", d) for d in range(2, nq)]
    for kind, d in order:
        for k in (1, 0):
            items.append((kind, k, d))

    for copy in selfs:
        copy.wait()
    for k in (0, 1):
        forward(k, q)

    def diag_item(item):
        kind, k, d = item
        s, ok = source(kind, k, d)

        @pl.when(ok)
        def _():
            diag_forward(k, s)

    lag = 4
    for t, (kind, k, d) in enumerate(items):
        s, ok = source(kind, k, d)

        @pl.when(ok)
        def _(kind=kind, k=k, s=s):
            (first_stop if kind == "first" else second_stop)(k, s)

        if t == 1:
            for kk in (0, 1):
                diag_forward(kk, q)
        if t >= lag:
            diag_item(items[t - lag])
    for item in items[max(0, len(items) - lag):]:
        diag_item(item)

    for p in range(4):
        qid[p, 0:1, :] = jnp.concatenate([IDS[4 * s + p, 2:3, :] for s in range(nq)], axis=1)
    row = jnp.concatenate([IDS[4 * s + r, k : k + 1, :] for k in (0, 1) for s in range(nq)], axis=1)
    colid[...] = jnp.broadcast_to(row, (128, 2 * rows)).T.reshape(colid.shape)
    racc[...] = jnp.full(racc.shape, FILL, F32)
    cacc[...] = jnp.full(cacc.shape, FILL, F32)

    @pl.loop(0, nq)
    def _(s):
        for k in (0, 1):
            parts(k, s)[2].wait()
            c_in(k, s).wait_recv()
            d_in(k, s).wait_recv()

    lane = lax.broadcasted_iota(jnp.int32, (cr2, 128), 1)
    sub = lax.broadcasted_iota(jnp.int32, (cr2, 128), 0)

    @pl.loop(0, 8 * nq)
    def _(step):
        p = step // (2 * nq)
        ks = lax.rem(step, 2 * nq)
        k, s = ks // nq, lax.rem(ks, nq)
        right = Q[p].reshape(rows, Q.shape[-1])
        scores = nt(A[k, s], right)
        col = colid[ks]
        own = jnp.where(k == 0, jnp.where(sub >= cr, 1, 0), jnp.where(sub < cr, 1, 0))
        own = jnp.where(p == r, own, 0)
        twin = jnp.where(own == 1, s * cr2 + sub + jnp.where(k == 0, -cr, cr), -1) - lane
        acc = racc[ks]
        for j in range(rows // 128):
            at = slice(128 * j, 128 * (j + 1))
            keep = jnp.logical_and(col == qid[p, 0:1, at], twin != 128 * j)
            block = jnp.where(keep, scores[:, at], FILL)
            acc = jnp.maximum(acc, block)
            cacc[p, 0:1, at] = jnp.maximum(cacc[p, 0:1, at], jnp.max(block, axis=0, keepdims=True))
        racc[ks] = acc

    best = jnp.max(racc[...].reshape(2 * rows, 128).T, axis=0, keepdims=True)
    fill = jnp.full((1, cr2), FILL, F32)
    for s in range(nq):
        for p in range(4):
            to = 4 * s + p
            same = p == r
            for k in (0, 1):
                at = (k * nq + s) * cr2
                MSG[to, k : k + 1, :] = jnp.where(same, best[:, at : at + cr2], fill)
            MSG[to, 2:3, :] = cacc[p, 0:1, cr2 * s : cr2 * (s + 1)]
            MSG[to, 3:8, :] = jnp.zeros((5, cr2), F32)

    def msg_copy(o):
        to = lax.rem(me + o, n)
        return remote(MSG.at[to], MSGR.at[me], msg_s.at[o], msg_r.at[me], to)

    @pl.loop(1, n)
    def _(o):
        msg_copy(o).start()

    MSGR[me] = MSG[me]

    for g in range(nq + 1):
        cond, copy = init(g)
        when(cond, copy.wait_send)

    @pl.loop(1, n)
    def _(o):
        ids_copy(o).wait_send()

    @pl.loop(0, nq)
    def _(s):
        for k in (0, 1):
            y, c, _ = parts(k, s)
            y.wait_send()
            c.wait_send()
            diag(k, s).wait_send()

    for kind, k, d in items:
        if kind == "first":
            s, ok = source(kind, k, d)

            @pl.when(jnp.logical_and(ok, jnp.logical_not(last[k])))
            def _(k=k, s=s):
                relay(k, s).wait_send()

    key = key_ref[...]
    bits = cr2.bit_length() - 1
    i0 = lax.broadcasted_iota(jnp.int32, (cr2, rows), 0)
    hot_q = jnp.where(i0 == (key & (cr2 - 1)), 1.0, 0.0).astype(BF16)
    hot_s = jnp.where(i0 == ((key + cr) & (cr2 - 1)), 1.0, 0.0).astype(BF16)
    at_q = lax.shift_right_logical(key, bits)
    at_s = lax.shift_right_logical(key + cr, bits)

    @pl.loop(1, n)
    def _(o):
        frm = lax.rem(me + o, n)
        remote(MSG.at[0], MSGR.at[frm], msg_s.at[o], msg_r.at[frm], frm).wait_recv()

    def top(s, k):
        found = MSGR[4 * s, k : k + 1, :]
        for p in range(1, 4):
            found = jnp.maximum(found, MSGR[4 * s + p, k : k + 1, :])
        return found

    segs = []
    for g in range(nq + 1):
        if g == 0:
            segs.append(top(0, 0))
        elif g == nq:
            segs.append(top(nq - 1, 1))
        else:
            segs.append(jnp.maximum(top(g, 0), top(g - 1, 1)))
    quads = [top(s, 2) for s in range(nq)]
    pad = -(-(nq + 1) // 8) * 8
    table_s = jnp.concatenate(segs + [fill] * (pad - nq - 1), axis=0)
    table_q = jnp.concatenate(quads + [fill] * (pad - nq), axis=0)
    which = lax.broadcasted_iota(jnp.int32, (pad, rows), 0)
    from_s = jnp.where(which == at_s, pick(table_s, hot_s), FILL)
    from_q = jnp.where(which == at_q, pick(table_q, hot_q), FILL)
    out_ref[...] = jnp.max(jnp.maximum(from_s, from_q), axis=0, keepdims=True)

    @pl.loop(1, n)
    def _(o):
        msg_copy(o).wait_send()


def body(n, embeddings, cluster_of, target_pos):
    rows, width = embeddings.shape
    piece = rows // n
    nq, cr = n // 4, 2 * piece
    assert MOST <= 4 * rows and n % 4 == 0
    vmem = pl.BlockSpec(memory_space=pltpu.VMEM)
    packed, idm, key = pl.pallas_call(
        functools.partial(pack_kernel, n),
        out_shape=(
            jax.ShapeDtypeStruct((rows + 2 * cr, width), BF16),
            jax.ShapeDtypeStruct((nq, 8, 2 * cr), jnp.int32),
            jax.ShapeDtypeStruct((1, rows), jnp.int32),
        ),
        in_specs=[vmem] * 3,
        out_specs=(vmem,) * 3,
        compiler_params=pltpu.CompilerParams(vmem_limit_bytes=40 * 2**20),
    )(embeddings, cluster_of.reshape(1, rows), target_pos.reshape(1, rows))
    dma = pltpu.SemaphoreType.DMA
    out = pl.pallas_call(
        functools.partial(main_kernel, n),
        out_shape=jax.ShapeDtypeStruct((1, rows), F32),
        in_specs=[vmem] * 3,
        out_specs=vmem,
        scratch_shapes=[
            pltpu.VMEM((2, nq, 2 * cr, width), BF16),
            pltpu.VMEM((4, nq, 2 * cr, width), BF16),
            pltpu.VMEM((n, 8, 2 * cr), jnp.int32),
            pltpu.VMEM((n, 8, 2 * cr), F32),
            pltpu.VMEM((n, 8, 2 * cr), F32),
            pltpu.VMEM((2 * nq, 2 * cr, 128), F32),
            pltpu.VMEM((4, 8, rows), F32),
            pltpu.VMEM((2 * nq, 2 * cr, 128), jnp.int32),
            pltpu.VMEM((4, 8, rows), jnp.int32),
            dma((nq + 1,)),
            dma((2, nq)), dma((2, nq)), dma((2, nq)), dma((2, nq)),
            dma((2, nq)), dma((2, nq)), dma((2, nq)), dma((2, nq)),
            dma((2, nq)), dma((2,)), dma((n,)), dma((n,)), dma((n,)), dma((n,)),
        ],
        compiler_params=pltpu.CompilerParams(
            collective_id=0, has_side_effects=True, vmem_limit_bytes=48 * 2**20
        ),
    )(packed.reshape(nq + 1, 2 * cr, width), idm, key)
    return out.reshape(rows)


def solution(mesh):
    n = mesh.shape["blk"] * mesh.shape["split"]
    spec = P(("groups", "blk", "split"))
    return jax.shard_map(
        functools.partial(body, n),
        mesh=mesh,
        in_specs=(P(("groups", "blk", "split"), None), spec, spec),
        out_specs=spec,
        check_vma=False,
    )
```

```python
import functools

import jax
import jax.numpy as jnp
from jax import lax
from jax.experimental import pallas as pl
from jax.experimental.pallas import tpu as pltpu
from jax.sharding import PartitionSpec as P

MOST = 4096
FILL = -4.0
MESH = pl.DeviceIdType.MESH
F32 = jnp.float32
BF16 = jnp.bfloat16


def nt(a, b):
    return lax.dot_general(a, b, (((1,), (1,)), ((), ())), preferred_element_type=F32)


def pack_kernel(n, emb, cl, tp, packed, idm, key_ref):
    rows, width = emb.shape
    piece = rows // n
    nq, cr = n // 4, 2 * piece
    shift = rows.bit_length() - 1
    x = emb[...].astype(F32)
    unit = (x * lax.rsqrt(jnp.sum(x * x, axis=1, keepdims=True) + 1e-06)).astype(BF16)
    dest = lax.shift_right_logical(tp[...], shift)
    hit = lax.broadcasted_iota(jnp.int32, (n, rows), 0) == dest
    hot = jnp.where(hit, 1.0, 0.0)
    i0 = lax.broadcasted_iota(jnp.int32, (rows, rows), 0)
    i1 = lax.broadcasted_iota(jnp.int32, (rows, rows), 1)
    before = jnp.where(i0 < i1, 1.0, 0.0).astype(BF16)
    counts = jnp.dot(hot.astype(BF16), before, preferred_element_type=F32)
    rank = jnp.sum(hot * counts, axis=0, keepdims=True).astype(jnp.int32)
    key = dest * piece + rank
    key_ref[...] = key
    perm = jnp.where(i0 == key, 1.0, 0.0).astype(BF16)
    zero = jnp.zeros((cr, width), BF16)
    packed[pl.ds(0, cr), :] = zero
    packed[pl.ds(cr, rows), :] = jnp.dot(perm, unit, preferred_element_type=F32).astype(BF16)
    packed[pl.ds(cr + rows, cr), :] = zero
    labels = jnp.broadcast_to(cl[...].astype(F32), (8, rows)).astype(BF16)
    ids = nt(labels, perm).astype(jnp.int32)[0:1]
    none = jnp.full((1, cr), -1, jnp.int32)
    padded = jnp.concatenate([none, ids, none], axis=1)
    for q in range(nq):
        idm[q, 0:1, :] = padded[:, 2 * cr * q : 2 * cr * (q + 1)]
        idm[q, 1:2, :] = padded[:, 2 * cr * (q + 1) : 2 * cr * (q + 2)]
        idm[q, 2:3, :] = ids[:, 2 * cr * q : 2 * cr * (q + 1)]
        idm[q, 3:8, :] = jnp.zeros((5, 2 * cr), jnp.int32)


def pick(table, hot):
    hi = table.astype(BF16)
    rest = table - hi.astype(F32)
    mid = rest.astype(BF16)
    low = (rest - mid.astype(F32)).astype(BF16)
    out = jnp.dot(hi, hot, preferred_element_type=F32)
    out += jnp.dot(mid, hot, preferred_element_type=F32)
    return out + jnp.dot(low, hot, preferred_element_type=F32)


def main_kernel(
    n, packed, idm, key_ref, out_ref,
    A, Q, IDS, MSG, MSGR, racc, cacc, colid, qid,
    init_s, recv, relay_s, y_s, y_r, c_s, c_r, d_s, d_r, loc, self_sem, ids_s, ids_r, msg_s, msg_r,
):
    nq = n // 4
    cr2 = packed.shape[1]
    cr = cr2 // 2
    rows = nq * cr2
    blk, split = lax.axis_index("blk"), lax.axis_index("split")
    me = blk * 2 + split
    q = blk // 2
    r = lax.rem(blk, 2) * 2 + split

    def dev(index):
        return {"blk": index // 2, "split": lax.rem(index, 2)}

    core = 4 * q + lax.rem(blk, 2) * 2 + (1 - split)
    across = 4 * q + lax.rem(r + 2, 4)
    rc = lax.rem(blk, 2) * 2 + (1 - split)
    ry = lax.rem(r + 2, 4)
    rd = lax.rem(rc + 2, 4)

    barrier = pltpu.get_barrier_semaphore()

    @pl.loop(1, n)
    def _(o):
        pl.semaphore_signal(
            barrier, inc=1, device_id=dev(lax.rem(me + o, n)), device_id_type=MESH
        )

    pl.semaphore_wait(barrier, n - 1)

    def remote(src, dst, s_sem, r_sem, index):
        return pltpu.make_async_remote_copy(
            src_ref=src, dst_ref=dst, send_sem=s_sem, recv_sem=r_sem,
            device_id=dev(index), device_id_type=MESH,
        )

    def ids_copy(o):
        to = lax.rem(me + o, n)
        return remote(idm.at[to // 4], IDS.at[me], ids_s.at[o], ids_r.at[me], to)

    def ids_in(o):
        frm = lax.rem(me + o, n)
        return remote(idm.at[0], IDS.at[frm], ids_s.at[o], ids_r.at[frm], frm)

    @pl.loop(1, n)
    def _(o):
        ids_copy(o).start()

    EDGE = {0: pl.ds(cr, cr), nq: pl.ds(0, cr)}

    def init(g):
        if g == 0:
            return q != 0, remote(
                packed.at[0, EDGE[0]], A.at[0, q, EDGE[0]], init_s.at[g], recv.at[0, q], r
            )
        if g == nq:
            return q != nq - 1, remote(
                packed.at[nq, EDGE[nq]], A.at[1, q, EDGE[nq]], init_s.at[g], recv.at[1, q],
                4 * (nq - 1) + r,
            )
        low = jnp.logical_or(q < g - 1, q == g)
        target = jnp.where(low, g - 1, g)
        side = g - target
        return None, remote(
            packed.at[g], A.at[side, q], init_s.at[g], recv.at[side, q], 4 * target + r
        )

    def when(cond, do):
        if cond is None:
            do()
        else:
            pl.when(cond)(do)

    def start_if(cond, g):
        pl.when(cond)(init(g)[1].start)

    for i in range(1, nq):
        start_if(q < nq - i - 1, nq - i)
        start_if(q > i, i)
    start_if(q != nq - 1, nq)
    start_if(q != 0, 0)
    for g in range(1, nq):
        start_if(jnp.logical_or(q == g, q == g - 1), g)

    selfs = [pltpu.make_async_copy(packed.at[q + k], A.at[k, q], self_sem.at[k]) for k in (0, 1)]
    for copy in selfs:
        copy.start()

    @pl.loop(1, n)
    def _(o):
        ids_in(o).wait_recv()

    IDS[me] = idm[q]

    def half(k):
        return pl.ds(pl.multiple_of(cr * (1 - k), cr), cr)

    def mine(k, s):
        return A.at[k, s, half(k)]

    def y_copy(k, s):
        return remote(mine(k, s), Q.at[s, k, r], y_s.at[k, s], y_r.at[k, s], across)

    def c_copy(k, s):
        return remote(mine(k, s), Q.at[s, k, r], c_s.at[k, s], c_r.at[k, s], core)

    def own_copy(k, s):
        return pltpu.make_async_copy(mine(k, s), Q.at[s, k, r], loc.at[k, s])

    def forward(k, s):
        y_copy(k, s).start()
        c_copy(k, s).start()
        own_copy(k, s).start()

    def y_in(k, s):
        return remote(mine(k, s), Q.at[s, k, ry], y_s.at[k, s], y_r.at[k, s], across)

    def diag(k, s):
        there = Q.at[s, k, ry]
        return remote(there, there, d_s.at[k, s], d_r.at[k, s], core)

    def c_in(k, s):
        return remote(mine(k, s), Q.at[s, k, rc], c_s.at[k, s], c_r.at[k, s], core)

    def d_in(k, s):
        there = Q.at[s, k, rd]
        return remote(there, there, d_s.at[k, s], d_r.at[k, s], core)

    def relay(k, s):
        to = me + 8 * k - 4
        return remote(A.at[k, s], A.at[1 - k, s], relay_s.at[k, s], recv.at[1 - k, s], to)

    def item(t):
        v = jnp.maximum(t - 2, 0)
        j = jnp.where(t < 2, 0, 1 + lax.rem(v, nq - 1))
        e = jnp.where(t < 2, t, v // (nq - 1))
        m = jnp.minimum(q, nq - 1 - q)
        d = (j + 1) // 2
        near = jnp.where(lax.rem(j, 2) == 1, q - d, q + d)
        far = jnp.where(q > nq - 1 - q, q - (j - m), q + (j - m))
        s = jnp.where(j <= 2 * m, near, far)
        return jnp.where(s < q, 1 - e, e), s, e

    def edge(k):
        return jnp.logical_or(
            jnp.logical_and(k == 1, q == nq - 1), jnp.logical_and(k == 0, q == 0)
        )

    def relays(k, s, e):
        return jnp.logical_and(
            jnp.logical_and(e == 0, s != q), jnp.logical_not(edge(k))
        )

    for p in range(4):
        for s in range(nq):
            for k in (0, 1):
                qid[2 * s + k, 0:1, cr * p : cr * (p + 1)] = IDS[
                    4 * s + p, 2:3, cr * k : cr * (k + 1)
                ]
    row = jnp.concatenate([IDS[4 * s + r, k : k + 1, :] for k in (0, 1) for s in range(nq)], axis=1)
    colid[...] = jnp.broadcast_to(row, (128, 2 * rows)).T.reshape(colid.shape)
    racc[...] = jnp.full(racc.shape, FILL, F32)
    cacc[...] = jnp.full(cacc.shape, FILL, F32)

    lane = lax.broadcasted_iota(jnp.int32, (cr2, 128), 1)
    sub = lax.broadcasted_iota(jnp.int32, (cr2, 128), 0)

    def tile(ta, tb):
        k, s, _ = item(ta)
        kb, sb, _ = item(tb)
        ks, at_b = k * nq + s, 2 * sb + kb
        scores = nt(A[k, s], Q[sb, kb].reshape(4 * cr, Q.shape[-1]))
        off = cr * (1 - k)
        own = jnp.logical_and(sub >= off, sub < off + cr)
        base = jnp.where(ta == tb, r * cr - off, -4 * rows)
        twin = jnp.where(own, sub + base, -1) - lane
        col = colid[ks]
        acc = racc[ks]
        for j in range(4 * cr // 128):
            at = slice(128 * j, 128 * (j + 1))
            keep = jnp.logical_and(col == qid[at_b, 0:1, at], twin != 128 * j)
            block = jnp.where(keep, scores[:, at], FILL)
            acc = jnp.maximum(acc, block)
            cacc[at_b, 0:1, at] = jnp.maximum(
                cacc[at_b, 0:1, at], jnp.max(block, axis=0, keepdims=True)
            )
        racc[ks] = acc

    for copy in selfs:
        copy.wait()

    @pl.loop(0, 2 * nq + 1)
    def _(t):
        @pl.when(t < 2 * nq)
        def _():
            k, s, e = item(t)

            @pl.when(s != q)
            def _():
                @pl.when(edge(k))
                def _():
                    remote(
                        packed.at[0, half(k)], mine(k, s), relay_s.at[k, s], recv.at[k, s], me
                    ).wait_recv()

                @pl.when(jnp.logical_not(edge(k)))
                def _():
                    remote(
                        packed.at[0], A.at[k, s], relay_s.at[k, s], recv.at[k, s], me
                    ).wait_recv()

            @pl.when(relays(k, s, e))
            def _():
                relay(k, s).start()

            forward(k, s)

        @pl.when(t > 0)
        def _():
            k, s, _ = item(t - 1)
            own_copy(k, s).wait()
            c_in(k, s).wait_recv()
            d_in(k, s).wait_recv()

            @pl.loop(0, t)
            def _(u):
                tile(u, t - 1)

        @pl.when(t < 2 * nq)
        def _():
            k, s, _ = item(t)
            y_in(k, s).wait_recv()
            diag(k, s).start()

            @pl.loop(0, t)
            def _(u):
                tile(t, u)

    best = jnp.max(racc[...].reshape(2 * rows, 128).T, axis=0, keepdims=True)
    fill = jnp.full((1, cr2), FILL, F32)
    for s in range(nq):
        for p in range(4):
            to = 4 * s + p
            same = p == r
            for k in (0, 1):
                at = (k * nq + s) * cr2
                MSG[to, k : k + 1, :] = jnp.where(same, best[:, at : at + cr2], fill)
            MSG[to, 2:3, :] = jnp.concatenate(
                [cacc[2 * s + k, 0:1, cr * p : cr * (p + 1)] for k in (0, 1)], axis=1
            )
            MSG[to, 3:8, :] = jnp.zeros((5, cr2), F32)

    def msg_copy(o):
        to = lax.rem(me + o, n)
        return remote(MSG.at[to], MSGR.at[me], msg_s.at[o], msg_r.at[me], to)

    @pl.loop(1, n)
    def _(o):
        msg_copy(o).start()

    MSGR[me] = MSG[me]

    for g in range(nq + 1):
        cond, copy = init(g)
        when(cond, copy.wait_send)

    @pl.loop(1, n)
    def _(o):
        ids_copy(o).wait_send()

    @pl.loop(0, 2 * nq)
    def _(t):
        k, s, e = item(t)
        y_copy(k, s).wait_send()
        c_copy(k, s).wait_send()
        diag(k, s).wait_send()

        @pl.when(relays(k, s, e))
        def _():
            relay(k, s).wait_send()

    key = key_ref[...]
    bits = cr2.bit_length() - 1
    i0 = lax.broadcasted_iota(jnp.int32, (cr2, rows), 0)
    hot_q = jnp.where(i0 == (key & (cr2 - 1)), 1.0, 0.0).astype(BF16)
    hot_s = jnp.where(i0 == ((key + cr) & (cr2 - 1)), 1.0, 0.0).astype(BF16)
    at_q = lax.shift_right_logical(key, bits)
    at_s = lax.shift_right_logical(key + cr, bits)

    @pl.loop(1, n)
    def _(o):
        frm = lax.rem(me + o, n)
        remote(MSG.at[0], MSGR.at[frm], msg_s.at[o], msg_r.at[frm], frm).wait_recv()

    def top(s, k):
        found = MSGR[4 * s, k : k + 1, :]
        for p in range(1, 4):
            found = jnp.maximum(found, MSGR[4 * s + p, k : k + 1, :])
        return found

    segs = []
    for g in range(nq + 1):
        if g == 0:
            segs.append(top(0, 0))
        elif g == nq:
            segs.append(top(nq - 1, 1))
        else:
            segs.append(jnp.maximum(top(g, 0), top(g - 1, 1)))
    quads = [top(s, 2) for s in range(nq)]
    pad = -(-(nq + 1) // 8) * 8
    table_s = jnp.concatenate(segs + [fill] * (pad - nq - 1), axis=0)
    table_q = jnp.concatenate(quads + [fill] * (pad - nq), axis=0)
    which = lax.broadcasted_iota(jnp.int32, (pad, rows), 0)
    from_s = jnp.where(which == at_s, pick(table_s, hot_s), FILL)
    from_q = jnp.where(which == at_q, pick(table_q, hot_q), FILL)
    out_ref[...] = jnp.max(jnp.maximum(from_s, from_q), axis=0, keepdims=True)

    @pl.loop(1, n)
    def _(o):
        msg_copy(o).wait_send()


def body(n, embeddings, cluster_of, target_pos):
    rows, width = embeddings.shape
    piece = rows // n
    nq, cr = n // 4, 2 * piece
    assert MOST <= 4 * rows and n % 4 == 0
    vmem = pl.BlockSpec(memory_space=pltpu.VMEM)
    packed, idm, key = pl.pallas_call(
        functools.partial(pack_kernel, n),
        out_shape=(
            jax.ShapeDtypeStruct((rows + 2 * cr, width), BF16),
            jax.ShapeDtypeStruct((nq, 8, 2 * cr), jnp.int32),
            jax.ShapeDtypeStruct((1, rows), jnp.int32),
        ),
        in_specs=[vmem] * 3,
        out_specs=(vmem,) * 3,
        compiler_params=pltpu.CompilerParams(vmem_limit_bytes=40 * 2**20),
    )(embeddings, cluster_of.reshape(1, rows), target_pos.reshape(1, rows))
    dma = pltpu.SemaphoreType.DMA
    out = pl.pallas_call(
        functools.partial(main_kernel, n),
        out_shape=jax.ShapeDtypeStruct((1, rows), F32),
        in_specs=[vmem] * 3,
        out_specs=vmem,
        scratch_shapes=[
            pltpu.VMEM((2, nq, 2 * cr, width), BF16),
            pltpu.VMEM((nq, 2, 4, cr, width), BF16),
            pltpu.VMEM((n, 8, 2 * cr), jnp.int32),
            pltpu.VMEM((n, 8, 2 * cr), F32),
            pltpu.VMEM((n, 8, 2 * cr), F32),
            pltpu.VMEM((2 * nq, 2 * cr, 128), F32),
            pltpu.VMEM((2 * nq, 8, 4 * cr), F32),
            pltpu.VMEM((2 * nq, 2 * cr, 128), jnp.int32),
            pltpu.VMEM((2 * nq, 8, 4 * cr), jnp.int32),
            dma((nq + 1,)),
            dma((2, nq)), dma((2, nq)), dma((2, nq)), dma((2, nq)),
            dma((2, nq)), dma((2, nq)), dma((2, nq)), dma((2, nq)),
            dma((2, nq)), dma((2,)), dma((n,)), dma((n,)), dma((n,)), dma((n,)),
        ],
        compiler_params=pltpu.CompilerParams(
            collective_id=0, has_side_effects=True, vmem_limit_bytes=48 * 2**20
        ),
    )(packed.reshape(nq + 1, 2 * cr, width), idm, key)
    return out.reshape(rows)


def solution(mesh):
    n = mesh.shape["blk"] * mesh.shape["split"]
    spec = P(("groups", "blk", "split"))
    return jax.shard_map(
        functools.partial(body, n),
        mesh=mesh,
        in_specs=(P(("groups", "blk", "split"), None), spec, spec),
        out_specs=spec,
        check_vma=False,
    )
```

```python
import functools

import jax
import jax.numpy as jnp
from jax import lax
from jax.experimental import pallas as pl
from jax.experimental.pallas import tpu as pltpu
from jax.sharding import PartitionSpec as P

MOST = 4096
FILL = -4.0
MESH = pl.DeviceIdType.MESH
F32 = jnp.float32
BF16 = jnp.bfloat16


def nt(a, b):
    return lax.dot_general(a, b, (((1,), (1,)), ((), ())), preferred_element_type=F32)


def pack_kernel(n, emb, cl, tp, packed, idm, key_ref):
    rows, width = emb.shape
    piece = rows // n
    nq, cr = n // 4, 2 * piece
    shift = rows.bit_length() - 1
    x = emb[...].astype(F32)
    unit = (x * lax.rsqrt(jnp.sum(x * x, axis=1, keepdims=True) + 1e-06)).astype(BF16)
    dest = lax.shift_right_logical(tp[...], shift)
    hit = lax.broadcasted_iota(jnp.int32, (n, rows), 0) == dest
    hot = jnp.where(hit, 1.0, 0.0)
    i0 = lax.broadcasted_iota(jnp.int32, (rows, rows), 0)
    i1 = lax.broadcasted_iota(jnp.int32, (rows, rows), 1)
    before = jnp.where(i0 < i1, 1.0, 0.0).astype(BF16)
    counts = jnp.dot(hot.astype(BF16), before, preferred_element_type=F32)
    rank = jnp.sum(hot * counts, axis=0, keepdims=True).astype(jnp.int32)
    key = dest * piece + rank
    key_ref[...] = key
    perm = jnp.where(i0 == key, 1.0, 0.0).astype(BF16)
    zero = jnp.zeros((cr, width), BF16)
    packed[pl.ds(0, cr), :] = zero
    packed[pl.ds(cr, rows), :] = jnp.dot(perm, unit, preferred_element_type=F32).astype(BF16)
    packed[pl.ds(cr + rows, cr), :] = zero
    labels = jnp.broadcast_to(cl[...].astype(F32), (8, rows)).astype(BF16)
    ids = nt(labels, perm).astype(jnp.int32)[0:1]
    none = jnp.full((1, cr), -1, jnp.int32)
    padded = jnp.concatenate([none, ids, none], axis=1)
    for q in range(nq):
        idm[q] = jnp.concatenate(
            [padded[:, 2 * cr * q : 2 * cr * (q + 2)], ids[:, 2 * cr * q : 2 * cr * (q + 1)]], axis=1
        )


def pick(table, hot):
    hi = table.astype(BF16)
    rest = table - hi.astype(F32)
    mid = rest.astype(BF16)
    low = (rest - mid.astype(F32)).astype(BF16)
    out = jnp.dot(hi, hot, preferred_element_type=F32)
    out += jnp.dot(mid, hot, preferred_element_type=F32)
    return out + jnp.dot(low, hot, preferred_element_type=F32)


def main_kernel(
    n, packed, idm, key_ref, out_ref,
    A, Q, IDS, MSG, MSGR, racc, cacc, colid, qid,
    init_s, recv, relay_s, y_s, y_r, c_s, c_r, d_s, d_r, loc, self_sem, ids_s, ids_r, msg_s, msg_r,
):
    nq = n // 4
    cr2 = packed.shape[1]
    cr = cr2 // 2
    rows = nq * cr2
    blk, split = lax.axis_index("blk"), lax.axis_index("split")
    me = blk * 2 + split
    q = blk // 2
    r = lax.rem(blk, 2) * 2 + split

    def dev(index):
        return {"blk": index // 2, "split": lax.rem(index, 2)}

    core = 4 * q + lax.rem(blk, 2) * 2 + (1 - split)
    across = 4 * q + lax.rem(r + 2, 4)
    rc = lax.rem(blk, 2) * 2 + (1 - split)
    ry = lax.rem(r + 2, 4)
    rd = lax.rem(rc + 2, 4)

    barrier = pltpu.get_barrier_semaphore()

    @pl.loop(1, n)
    def _(o):
        pl.semaphore_signal(
            barrier, inc=1, device_id=dev(lax.rem(me + o, n)), device_id_type=MESH
        )

    pl.semaphore_wait(barrier, n - 1)

    def remote(src, dst, s_sem, r_sem, index):
        return pltpu.make_async_remote_copy(
            src_ref=src, dst_ref=dst, send_sem=s_sem, recv_sem=r_sem,
            device_id=dev(index), device_id_type=MESH,
        )

    def ids_copy(o):
        to = lax.rem(me + o, n)
        return remote(idm.at[to // 4], IDS.at[me], ids_s.at[o], ids_r.at[me], to)

    def ids_in(o):
        frm = lax.rem(me + o, n)
        return remote(idm.at[0], IDS.at[frm], ids_s.at[o], ids_r.at[frm], frm)

    @pl.loop(1, n)
    def _(o):
        ids_copy(o).start()

    EDGE = {0: pl.ds(cr, cr), nq: pl.ds(0, cr)}

    def init(g):
        if g == 0:
            return q != 0, remote(
                packed.at[0, EDGE[0]], A.at[0, q, EDGE[0]], init_s.at[g], recv.at[0, q], r
            )
        if g == nq:
            return q != nq - 1, remote(
                packed.at[nq, EDGE[nq]], A.at[1, q, EDGE[nq]], init_s.at[g], recv.at[1, q],
                4 * (nq - 1) + r,
            )
        low = jnp.logical_or(q < g - 1, q == g)
        target = jnp.where(low, g - 1, g)
        side = g - target
        return None, remote(
            packed.at[g], A.at[side, q], init_s.at[g], recv.at[side, q], 4 * target + r
        )

    def when(cond, do):
        if cond is None:
            do()
        else:
            pl.when(cond)(do)

    def start_if(cond, g):
        pl.when(cond)(init(g)[1].start)

    for i in range(1, nq):
        start_if(q < nq - i - 1, nq - i)
        start_if(q > i, i)
    start_if(q != nq - 1, nq)
    start_if(q != 0, 0)
    for g in range(1, nq):
        start_if(jnp.logical_or(q == g, q == g - 1), g)

    selfs = [pltpu.make_async_copy(packed.at[q + k], A.at[k, q], self_sem.at[k]) for k in (0, 1)]
    for copy in selfs:
        copy.start()

    @pl.loop(1, n)
    def _(o):
        ids_in(o).wait_recv()

    IDS[me] = idm[q]

    def half(k):
        return pl.ds(pl.multiple_of(cr * (1 - k), cr), cr)

    def mine(k, s):
        return A.at[k, s, half(k)]

    def y_copy(k, s):
        return remote(mine(k, s), Q.at[s, k, r], y_s.at[k, s], y_r.at[k, s], across)

    def c_copy(k, s):
        return remote(mine(k, s), Q.at[s, k, r], c_s.at[k, s], c_r.at[k, s], core)

    def own_copy(k, s):
        return pltpu.make_async_copy(mine(k, s), Q.at[s, k, r], loc.at[k, s])

    def forward(k, s):
        y_copy(k, s).start()
        c_copy(k, s).start()
        own_copy(k, s).start()

    def y_in(k, s):
        return remote(mine(k, s), Q.at[s, k, ry], y_s.at[k, s], y_r.at[k, s], across)

    def diag(k, s):
        there = Q.at[s, k, ry]
        return remote(there, there, d_s.at[k, s], d_r.at[k, s], core)

    def c_in(k, s):
        return remote(mine(k, s), Q.at[s, k, rc], c_s.at[k, s], c_r.at[k, s], core)

    def d_in(k, s):
        there = Q.at[s, k, rd]
        return remote(there, there, d_s.at[k, s], d_r.at[k, s], core)

    def relay(k, s):
        to = me + 8 * k - 4
        return remote(A.at[k, s], A.at[1 - k, s], relay_s.at[k, s], recv.at[1 - k, s], to)

    def item(t):
        v = jnp.maximum(t - 2, 0)
        j = jnp.where(t < 2, 0, 1 + lax.rem(v, nq - 1))
        e = jnp.where(t < 2, t, v // (nq - 1))
        m = jnp.minimum(q, nq - 1 - q)
        d = (j + 1) // 2
        near = jnp.where(lax.rem(j, 2) == 1, q - d, q + d)
        far = jnp.where(q > nq - 1 - q, q - (j - m), q + (j - m))
        s = jnp.where(j <= 2 * m, near, far)
        return jnp.where(s < q, 1 - e, e), s, e

    def edge(k):
        return jnp.logical_or(
            jnp.logical_and(k == 1, q == nq - 1), jnp.logical_and(k == 0, q == 0)
        )

    def relays(k, s, e):
        return jnp.logical_and(
            jnp.logical_and(e == 0, s != q), jnp.logical_not(edge(k))
        )

    for p in range(4):
        for s in range(nq):
            for k in (0, 1):
                qid[2 * s + k, 0:1, cr * p : cr * (p + 1)] = IDS[
                    4 * s + p, :, 2 * cr2 + cr * k : 2 * cr2 + cr * (k + 1)
                ]
    row = jnp.concatenate([IDS[4 * s + r, :, k * cr2 : (k + 1) * cr2] for k in (0, 1) for s in range(nq)], axis=1)
    colid[...] = jnp.broadcast_to(row, (128, 2 * rows)).T.reshape(colid.shape)
    racc[...] = jnp.full(racc.shape, FILL, F32)
    cacc[...] = jnp.full(cacc.shape, FILL, F32)

    lane = lax.broadcasted_iota(jnp.int32, (cr2, 128), 1)
    sub = lax.broadcasted_iota(jnp.int32, (cr2, 128), 0)

    def tile(ta, tb):
        k, s, _ = item(ta)
        kb, sb, _ = item(tb)
        ks, at_b = k * nq + s, 2 * sb + kb
        scores = nt(A[k, s], Q[sb, kb].reshape(4 * cr, Q.shape[-1]))
        off = cr * (1 - k)
        own = jnp.logical_and(sub >= off, sub < off + cr)
        base = jnp.where(ta == tb, r * cr - off, -4 * rows)
        twin = jnp.where(own, sub + base, -1) - lane
        col = colid[ks]
        acc = racc[ks]
        for j in range(4 * cr // 128):
            at = slice(128 * j, 128 * (j + 1))
            keep = jnp.logical_and(col == qid[at_b, 0:1, at], twin != 128 * j)
            block = jnp.where(keep, scores[:, at], FILL)
            acc = jnp.maximum(acc, block)
            cacc[at_b, 0:1, at] = jnp.maximum(
                cacc[at_b, 0:1, at], jnp.max(block, axis=0, keepdims=True)
            )
        racc[ks] = acc

    for copy in selfs:
        copy.wait()

    @pl.loop(0, 2 * nq + 2)
    def _(t):
        @pl.when(t < 2 * nq)
        def _():
            k, s, e = item(t)

            @pl.when(s != q)
            def _():
                @pl.when(edge(k))
                def _():
                    remote(
                        packed.at[0, half(k)], mine(k, s), relay_s.at[k, s], recv.at[k, s], me
                    ).wait_recv()

                @pl.when(jnp.logical_not(edge(k)))
                def _():
                    remote(
                        packed.at[0], A.at[k, s], relay_s.at[k, s], recv.at[k, s], me
                    ).wait_recv()

            @pl.when(relays(k, s, e))
            def _():
                relay(k, s).start()

            forward(k, s)

        @pl.when(jnp.logical_and(t >= 1, t < 2 * nq + 1))
        def _():
            k, s, _ = item(t - 1)
            y_in(k, s).wait_recv()
            diag(k, s).start()

        @pl.when(t >= 2)
        def _():
            k, s, _ = item(t - 2)
            own_copy(k, s).wait()
            c_in(k, s).wait_recv()
            d_in(k, s).wait_recv()

            @pl.loop(0, jnp.minimum(t + 1, 2 * nq))
            def _(u):
                tile(u, t - 2)

        @pl.when(jnp.logical_and(t >= 3, t < 2 * nq))
        def _():
            @pl.loop(0, t - 2)
            def _(u):
                tile(t, u)

    best = jnp.max(racc[...].reshape(2 * rows, 128).T, axis=0, keepdims=True)
    fill = jnp.full((1, cr2), FILL, F32)
    for s in range(nq):
        for p in range(4):
            to = 4 * s + p
            same = p == r
            found = [best[:, (k * nq + s) * cr2 : (k * nq + s + 1) * cr2] for k in (0, 1)]
            found = [jnp.where(same, one, fill) for one in found]
            found += [cacc[2 * s + k, 0:1, cr * p : cr * (p + 1)] for k in (0, 1)]
            MSG[to] = jnp.concatenate(found, axis=1)

    def msg_copy(o):
        to = lax.rem(me + o, n)
        return remote(MSG.at[to], MSGR.at[me], msg_s.at[o], msg_r.at[me], to)

    @pl.loop(1, n)
    def _(o):
        msg_copy(o).start()

    MSGR[me] = MSG[me]

    for g in range(nq + 1):
        cond, copy = init(g)
        when(cond, copy.wait_send)

    @pl.loop(1, n)
    def _(o):
        ids_copy(o).wait_send()

    @pl.loop(0, 2 * nq)
    def _(t):
        k, s, e = item(t)
        y_copy(k, s).wait_send()
        c_copy(k, s).wait_send()
        diag(k, s).wait_send()

        @pl.when(relays(k, s, e))
        def _():
            relay(k, s).wait_send()

    key = key_ref[...]
    bits = cr2.bit_length() - 1
    i0 = lax.broadcasted_iota(jnp.int32, (cr2, rows), 0)
    hot_q = jnp.where(i0 == (key & (cr2 - 1)), 1.0, 0.0).astype(BF16)
    hot_s = jnp.where(i0 == ((key + cr) & (cr2 - 1)), 1.0, 0.0).astype(BF16)
    at_q = lax.shift_right_logical(key, bits)
    at_s = lax.shift_right_logical(key + cr, bits)

    @pl.loop(1, n)
    def _(o):
        frm = lax.rem(me + o, n)
        remote(MSG.at[0], MSGR.at[frm], msg_s.at[o], msg_r.at[frm], frm).wait_recv()

    def top(s, k):
        found = MSGR[4 * s, :, k * cr2 : (k + 1) * cr2]
        for p in range(1, 4):
            found = jnp.maximum(found, MSGR[4 * s + p, :, k * cr2 : (k + 1) * cr2])
        return found

    segs = []
    for g in range(nq + 1):
        if g == 0:
            segs.append(top(0, 0))
        elif g == nq:
            segs.append(top(nq - 1, 1))
        else:
            segs.append(jnp.maximum(top(g, 0), top(g - 1, 1)))
    quads = [top(s, 2) for s in range(nq)]
    pad = -(-(nq + 1) // 8) * 8
    table_s = jnp.concatenate(segs + [fill] * (pad - nq - 1), axis=0)
    table_q = jnp.concatenate(quads + [fill] * (pad - nq), axis=0)
    which = lax.broadcasted_iota(jnp.int32, (pad, rows), 0)
    from_s = jnp.where(which == at_s, pick(table_s, hot_s), FILL)
    from_q = jnp.where(which == at_q, pick(table_q, hot_q), FILL)
    out_ref[...] = jnp.max(jnp.maximum(from_s, from_q), axis=0, keepdims=True)

    @pl.loop(1, n)
    def _(o):
        msg_copy(o).wait_send()


def body(n, embeddings, cluster_of, target_pos):
    rows, width = embeddings.shape
    piece = rows // n
    nq, cr = n // 4, 2 * piece
    assert MOST <= 4 * rows and n % 4 == 0
    vmem = pl.BlockSpec(memory_space=pltpu.VMEM)
    packed, idm, key = pl.pallas_call(
        functools.partial(pack_kernel, n),
        out_shape=(
            jax.ShapeDtypeStruct((rows + 2 * cr, width), BF16),
            jax.ShapeDtypeStruct((nq, 1, 6 * cr), jnp.int32),
            jax.ShapeDtypeStruct((1, rows), jnp.int32),
        ),
        in_specs=[vmem] * 3,
        out_specs=(vmem,) * 3,
        compiler_params=pltpu.CompilerParams(vmem_limit_bytes=40 * 2**20),
    )(embeddings, cluster_of.reshape(1, rows), target_pos.reshape(1, rows))
    dma = pltpu.SemaphoreType.DMA
    out = pl.pallas_call(
        functools.partial(main_kernel, n),
        out_shape=jax.ShapeDtypeStruct((1, rows), F32),
        in_specs=[vmem] * 3,
        out_specs=vmem,
        scratch_shapes=[
            pltpu.VMEM((2, nq, 2 * cr, width), BF16),
            pltpu.VMEM((nq, 2, 4, cr, width), BF16),
            pltpu.VMEM((n, 1, 6 * cr), jnp.int32),
            pltpu.VMEM((n, 1, 6 * cr), F32),
            pltpu.VMEM((n, 1, 6 * cr), F32),
            pltpu.VMEM((2 * nq, 2 * cr, 128), F32),
            pltpu.VMEM((2 * nq, 8, 4 * cr), F32),
            pltpu.VMEM((2 * nq, 2 * cr, 128), jnp.int32),
            pltpu.VMEM((2 * nq, 8, 4 * cr), jnp.int32),
            dma((nq + 1,)),
            dma((2, nq)), dma((2, nq)), dma((2, nq)), dma((2, nq)),
            dma((2, nq)), dma((2, nq)), dma((2, nq)), dma((2, nq)),
            dma((2, nq)), dma((2,)), dma((n,)), dma((n,)), dma((n,)), dma((n,)),
        ],
        compiler_params=pltpu.CompilerParams(
            collective_id=0, has_side_effects=True, vmem_limit_bytes=48 * 2**20
        ),
    )(packed.reshape(nq + 1, 2 * cr, width), idm, key)
    return out.reshape(rows)


def solution(mesh):
    n = mesh.shape["blk"] * mesh.shape["split"]
    spec = P(("groups", "blk", "split"))
    return jax.shard_map(
        functools.partial(body, n),
        mesh=mesh,
        in_specs=(P(("groups", "blk", "split"), None), spec, spec),
        out_specs=spec,
        check_vma=False,
    )
```

```python
import functools

import jax
import jax.numpy as jnp
from jax import lax
from jax.experimental import pallas as pl
from jax.experimental.pallas import tpu as pltpu
from jax.sharding import PartitionSpec as P

MOST = 4096
FILL = -4.0
MESH = pl.DeviceIdType.MESH
F32 = jnp.float32
BF16 = jnp.bfloat16


def nt(a, b):
    return lax.dot_general(a, b, (((1,), (1,)), ((), ())), preferred_element_type=F32)


def pack_kernel(n, emb_in, cl_in, tp_in, packed, idm, key_ref, emb, cl, tp, sem):
    fetch = [
        pltpu.make_async_copy(src, dst, sem.at[i])
        for i, (src, dst) in enumerate(((tp_in, tp), (cl_in, cl), (emb_in, emb)))
    ]
    for copy in fetch:
        copy.start()
    rows, width = emb.shape
    piece = rows // n
    nq, cr = n // 4, 2 * piece
    shift = rows.bit_length() - 1
    fetch[0].wait()
    dest = lax.shift_right_logical(tp[...], shift)
    hit = lax.broadcasted_iota(jnp.int32, (n, rows), 0) == dest
    hot = jnp.where(hit, 1.0, 0.0)
    i0 = lax.broadcasted_iota(jnp.int32, (rows, rows), 0)
    i1 = lax.broadcasted_iota(jnp.int32, (rows, rows), 1)
    before = jnp.where(i0 < i1, 1.0, 0.0).astype(BF16)
    counts = jnp.dot(hot.astype(BF16), before, preferred_element_type=F32)
    rank = jnp.sum(hot * counts, axis=0, keepdims=True).astype(jnp.int32)
    key = dest * piece + rank
    key_ref[...] = key
    perm = jnp.where(i0 == key, 1.0, 0.0).astype(BF16)
    zero = jnp.zeros((cr, width), BF16)
    fetch[2].wait()
    x = emb[...].astype(F32)
    unit = (x * lax.rsqrt(jnp.sum(x * x, axis=1, keepdims=True) + 1e-06)).astype(BF16)
    packed[pl.ds(0, cr), :] = zero
    packed[pl.ds(cr, rows), :] = jnp.dot(perm, unit, preferred_element_type=F32).astype(BF16)
    packed[pl.ds(cr + rows, cr), :] = zero
    fetch[1].wait()
    labels = jnp.broadcast_to(cl[...].astype(F32), (8, rows)).astype(BF16)
    ids = nt(labels, perm).astype(jnp.int32)[0:1]
    none = jnp.full((1, cr), -1, jnp.int32)
    padded = jnp.concatenate([none, ids, none], axis=1)
    for q in range(nq):
        idm[q] = jnp.concatenate(
            [padded[:, 2 * cr * q : 2 * cr * (q + 2)], ids[:, 2 * cr * q : 2 * cr * (q + 1)]], axis=1
        )


def pick(table, hot):
    hi = table.astype(BF16)
    rest = table - hi.astype(F32)
    mid = rest.astype(BF16)
    low = (rest - mid.astype(F32)).astype(BF16)
    out = jnp.dot(hi, hot, preferred_element_type=F32)
    out += jnp.dot(mid, hot, preferred_element_type=F32)
    return out + jnp.dot(low, hot, preferred_element_type=F32)


def main_kernel(
    n, packed, idm, key_ref, out_ref,
    A, Q, IDS, MSG, MSGR, racc, cacc, colid, qid,
    init_s, recv, relay_s, y_s, y_r, c_s, c_r, d_s, d_r, loc, self_sem, ids_s, ids_r, msg_s, msg_r,
):
    nq = n // 4
    cr2 = packed.shape[1]
    cr = cr2 // 2
    rows = nq * cr2
    blk, split = lax.axis_index("blk"), lax.axis_index("split")
    me = blk * 2 + split
    q = blk // 2
    r = lax.rem(blk, 2) * 2 + split

    def dev(index):
        return {"blk": index // 2, "split": lax.rem(index, 2)}

    core = 4 * q + lax.rem(blk, 2) * 2 + (1 - split)
    across = 4 * q + lax.rem(r + 2, 4)
    rc = lax.rem(blk, 2) * 2 + (1 - split)
    ry = lax.rem(r + 2, 4)
    rd = lax.rem(rc + 2, 4)

    barrier = pltpu.get_barrier_semaphore()

    @pl.loop(1, n)
    def _(o):
        pl.semaphore_signal(
            barrier, inc=1, device_id=dev(lax.rem(me + o, n)), device_id_type=MESH
        )

    pl.semaphore_wait(barrier, n - 1)

    def remote(src, dst, s_sem, r_sem, index):
        return pltpu.make_async_remote_copy(
            src_ref=src, dst_ref=dst, send_sem=s_sem, recv_sem=r_sem,
            device_id=dev(index), device_id_type=MESH,
        )

    def ids_copy(o):
        to = lax.rem(me + o, n)
        return remote(idm.at[to // 4], IDS.at[me], ids_s.at[o], ids_r.at[me], to)

    def ids_in(o):
        frm = lax.rem(me + o, n)
        return remote(idm.at[0], IDS.at[frm], ids_s.at[o], ids_r.at[frm], frm)

    @pl.loop(1, n)
    def _(o):
        ids_copy(o).start()

    EDGE = {0: pl.ds(cr, cr), nq: pl.ds(0, cr)}

    def init(g):
        if g == 0:
            return q != 0, remote(
                packed.at[0, EDGE[0]], A.at[0, q, EDGE[0]], init_s.at[g], recv.at[0, q], r
            )
        if g == nq:
            return q != nq - 1, remote(
                packed.at[nq, EDGE[nq]], A.at[1, q, EDGE[nq]], init_s.at[g], recv.at[1, q],
                4 * (nq - 1) + r,
            )
        low = jnp.logical_or(q < g - 1, q == g)
        target = jnp.where(low, g - 1, g)
        side = g - target
        return None, remote(
            packed.at[g], A.at[side, q], init_s.at[g], recv.at[side, q], 4 * target + r
        )

    def when(cond, do):
        if cond is None:
            do()
        else:
            pl.when(cond)(do)

    def start_if(cond, g):
        pl.when(cond)(init(g)[1].start)

    for i in range(1, nq):
        start_if(q < nq - i - 1, nq - i)
        start_if(q > i, i)
    start_if(q != nq - 1, nq)
    start_if(q != 0, 0)
    for g in range(1, nq):
        start_if(jnp.logical_or(q == g, q == g - 1), g)

    selfs = [pltpu.make_async_copy(packed.at[q + k], A.at[k, q], self_sem.at[k]) for k in (0, 1)]
    for copy in selfs:
        copy.start()

    @pl.loop(1, n)
    def _(o):
        ids_in(o).wait_recv()

    IDS[me] = idm[q]

    def half(k):
        return pl.ds(pl.multiple_of(cr * (1 - k), cr), cr)

    def mine(k, s):
        return A.at[k, s, half(k)]

    def y_copy(k, s):
        return remote(mine(k, s), Q.at[s, k, r], y_s.at[k, s], y_r.at[k, s], across)

    def c_copy(k, s):
        return remote(mine(k, s), Q.at[s, k, r], c_s.at[k, s], c_r.at[k, s], core)

    def own_copy(k, s):
        return pltpu.make_async_copy(mine(k, s), Q.at[s, k, r], loc.at[k, s])

    def forward(k, s):
        y_copy(k, s).start()
        c_copy(k, s).start()
        own_copy(k, s).start()

    def y_in(k, s):
        return remote(mine(k, s), Q.at[s, k, ry], y_s.at[k, s], y_r.at[k, s], across)

    def diag(k, s):
        there = Q.at[s, k, ry]
        return remote(there, there, d_s.at[k, s], d_r.at[k, s], core)

    def c_in(k, s):
        return remote(mine(k, s), Q.at[s, k, rc], c_s.at[k, s], c_r.at[k, s], core)

    def d_in(k, s):
        there = Q.at[s, k, rd]
        return remote(there, there, d_s.at[k, s], d_r.at[k, s], core)

    def relay(k, s):
        to = me + 8 * k - 4
        return remote(A.at[k, s], A.at[1 - k, s], relay_s.at[k, s], recv.at[1 - k, s], to)

    def item(t):
        v = jnp.maximum(t - 2, 0)
        j = jnp.where(t < 2, 0, 1 + lax.rem(v, nq - 1))
        e = jnp.where(t < 2, t, v // (nq - 1))
        m = jnp.minimum(q, nq - 1 - q)
        d = (j + 1) // 2
        near = jnp.where(lax.rem(j, 2) == 1, q - d, q + d)
        far = jnp.where(q > nq - 1 - q, q - (j - m), q + (j - m))
        s = jnp.where(j <= 2 * m, near, far)
        return jnp.where(s < q, 1 - e, e), s, e

    def edge(k):
        return jnp.logical_or(
            jnp.logical_and(k == 1, q == nq - 1), jnp.logical_and(k == 0, q == 0)
        )

    def relays(k, s, e):
        return jnp.logical_and(
            jnp.logical_and(e == 0, s != q), jnp.logical_not(edge(k))
        )

    for p in range(4):
        for s in range(nq):
            for k in (0, 1):
                qid[2 * s + k, 0:1, cr * p : cr * (p + 1)] = IDS[
                    4 * s + p, :, 2 * cr2 + cr * k : 2 * cr2 + cr * (k + 1)
                ]
    row = jnp.concatenate([IDS[4 * s + r, :, k * cr2 : (k + 1) * cr2] for k in (0, 1) for s in range(nq)], axis=1)
    colid[...] = jnp.broadcast_to(row, (128, 2 * rows)).T.reshape(colid.shape)
    racc[...] = jnp.full(racc.shape, FILL, F32)
    cacc[...] = jnp.full(cacc.shape, FILL, F32)

    lane = lax.broadcasted_iota(jnp.int32, (cr2, 128), 1)
    sub = lax.broadcasted_iota(jnp.int32, (cr2, 128), 0)

    def scores_of(ta, tb):
        k, s, _ = item(ta)
        kb, sb, _ = item(tb)
        return nt(A[k, s], Q[sb, kb].reshape(4 * cr, Q.shape[-1]))

    def take(ta, tb, scores):
        k, s, _ = item(ta)
        kb, sb, _ = item(tb)
        ks, at_b = k * nq + s, 2 * sb + kb
        off = cr * (1 - k)
        own = jnp.logical_and(sub >= off, sub < off + cr)
        base = jnp.where(ta == tb, r * cr - off, -4 * rows)
        twin = jnp.where(own, sub + base, -1) - lane
        col = colid[ks]
        acc = racc[ks]
        for j in range(4 * cr // 128):
            at = slice(128 * j, 128 * (j + 1))
            keep = jnp.logical_and(col == qid[at_b, 0:1, at], twin != 128 * j)
            block = jnp.where(keep, scores[:, at], FILL)
            acc = jnp.maximum(acc, block)
            cacc[at_b, 0:1, at] = jnp.maximum(
                cacc[at_b, 0:1, at], jnp.max(block, axis=0, keepdims=True)
            )
        racc[ks] = acc

    def tiles(count, pair):
        @pl.loop(0, (count + 1) // 2)
        def _(i):
            one, two = pair(2 * i), pair(jnp.minimum(2 * i + 1, count - 1))
            first, second = scores_of(*one), scores_of(*two)
            take(*one, first)
            take(*two, second)

    for copy in selfs:
        copy.wait()

    @pl.loop(0, 2 * nq + 2)
    def _(t):
        @pl.when(t < 2 * nq)
        def _():
            k, s, e = item(t)

            @pl.when(s != q)
            def _():
                @pl.when(edge(k))
                def _():
                    remote(
                        packed.at[0, half(k)], mine(k, s), relay_s.at[k, s], recv.at[k, s], me
                    ).wait_recv()

                @pl.when(jnp.logical_not(edge(k)))
                def _():
                    remote(
                        packed.at[0], A.at[k, s], relay_s.at[k, s], recv.at[k, s], me
                    ).wait_recv()

            @pl.when(relays(k, s, e))
            def _():
                relay(k, s).start()

            forward(k, s)

        @pl.when(jnp.logical_and(t >= 1, t < 2 * nq + 1))
        def _():
            k, s, _ = item(t - 1)
            y_in(k, s).wait_recv()
            diag(k, s).start()

        @pl.when(t >= 2)
        def _():
            k, s, _ = item(t - 2)
            own_copy(k, s).wait()
            c_in(k, s).wait_recv()
            d_in(k, s).wait_recv()

            tiles(jnp.minimum(t + 1, 2 * nq), lambda u: (u, t - 2))

        @pl.when(jnp.logical_and(t >= 3, t < 2 * nq))
        def _():
            tiles(t - 2, lambda u: (t, u))

    best = jnp.max(racc[...].reshape(2 * rows, 128).T, axis=0, keepdims=True)
    fill = jnp.full((1, cr2), FILL, F32)
    for s in range(nq):
        for p in range(4):
            to = 4 * s + p
            same = p == r
            found = [best[:, (k * nq + s) * cr2 : (k * nq + s + 1) * cr2] for k in (0, 1)]
            found = [jnp.where(same, one, fill) for one in found]
            found += [cacc[2 * s + k, 0:1, cr * p : cr * (p + 1)] for k in (0, 1)]
            MSG[to] = jnp.concatenate(found, axis=1)

    def msg_copy(o):
        to = lax.rem(me + o, n)
        return remote(MSG.at[to], MSGR.at[me], msg_s.at[o], msg_r.at[me], to)

    @pl.loop(1, n)
    def _(o):
        msg_copy(o).start()

    MSGR[me] = MSG[me]

    for g in range(nq + 1):
        cond, copy = init(g)
        when(cond, copy.wait_send)

    @pl.loop(1, n)
    def _(o):
        ids_copy(o).wait_send()

    @pl.loop(0, 2 * nq)
    def _(t):
        k, s, e = item(t)
        y_copy(k, s).wait_send()
        c_copy(k, s).wait_send()
        diag(k, s).wait_send()

        @pl.when(relays(k, s, e))
        def _():
            relay(k, s).wait_send()

    key = key_ref[...]
    bits = cr2.bit_length() - 1
    i0 = lax.broadcasted_iota(jnp.int32, (cr2, rows), 0)
    hot_q = jnp.where(i0 == (key & (cr2 - 1)), 1.0, 0.0).astype(BF16)
    hot_s = jnp.where(i0 == ((key + cr) & (cr2 - 1)), 1.0, 0.0).astype(BF16)
    at_q = lax.shift_right_logical(key, bits)
    at_s = lax.shift_right_logical(key + cr, bits)

    @pl.loop(1, n)
    def _(o):
        frm = lax.rem(me + o, n)
        remote(MSG.at[0], MSGR.at[frm], msg_s.at[o], msg_r.at[frm], frm).wait_recv()

    def top(s, k):
        found = MSGR[4 * s, :, k * cr2 : (k + 1) * cr2]
        for p in range(1, 4):
            found = jnp.maximum(found, MSGR[4 * s + p, :, k * cr2 : (k + 1) * cr2])
        return found

    segs = []
    for g in range(nq + 1):
        if g == 0:
            segs.append(top(0, 0))
        elif g == nq:
            segs.append(top(nq - 1, 1))
        else:
            segs.append(jnp.maximum(top(g, 0), top(g - 1, 1)))
    quads = [top(s, 2) for s in range(nq)]
    pad = -(-(nq + 1) // 8) * 8
    table_s = jnp.concatenate(segs + [fill] * (pad - nq - 1), axis=0)
    table_q = jnp.concatenate(quads + [fill] * (pad - nq), axis=0)
    which = lax.broadcasted_iota(jnp.int32, (pad, rows), 0)
    from_s = jnp.where(which == at_s, pick(table_s, hot_s), FILL)
    from_q = jnp.where(which == at_q, pick(table_q, hot_q), FILL)
    out_ref[...] = jnp.max(jnp.maximum(from_s, from_q), axis=0, keepdims=True)

    @pl.loop(1, n)
    def _(o):
        msg_copy(o).wait_send()


def body(n, embeddings, cluster_of, target_pos):
    rows, width = embeddings.shape
    piece = rows // n
    nq, cr = n // 4, 2 * piece
    assert MOST <= 4 * rows and n % 4 == 0
    vmem = pl.BlockSpec(memory_space=pltpu.VMEM)
    packed, idm, key = pl.pallas_call(
        functools.partial(pack_kernel, n),
        out_shape=(
            jax.ShapeDtypeStruct((rows + 2 * cr, width), BF16),
            jax.ShapeDtypeStruct((nq, 1, 6 * cr), jnp.int32),
            jax.ShapeDtypeStruct((1, rows), jnp.int32),
        ),
        in_specs=[pl.BlockSpec(memory_space=pl.ANY)] * 3,
        out_specs=(vmem,) * 3,
        scratch_shapes=[
            pltpu.VMEM((rows, width), BF16),
            pltpu.VMEM((1, rows), jnp.int32),
            pltpu.VMEM((1, rows), jnp.int32),
            pltpu.SemaphoreType.DMA((3,)),
        ],
        compiler_params=pltpu.CompilerParams(vmem_limit_bytes=40 * 2**20),
    )(embeddings, cluster_of.reshape(1, rows), target_pos.reshape(1, rows))
    dma = pltpu.SemaphoreType.DMA
    out = pl.pallas_call(
        functools.partial(main_kernel, n),
        out_shape=jax.ShapeDtypeStruct((1, rows), F32),
        in_specs=[vmem] * 3,
        out_specs=vmem,
        scratch_shapes=[
            pltpu.VMEM((2, nq, 2 * cr, width), BF16),
            pltpu.VMEM((nq, 2, 4, cr, width), BF16),
            pltpu.VMEM((n, 1, 6 * cr), jnp.int32),
            pltpu.VMEM((n, 1, 6 * cr), F32),
            pltpu.VMEM((n, 1, 6 * cr), F32),
            pltpu.VMEM((2 * nq, 2 * cr, 128), F32),
            pltpu.VMEM((2 * nq, 8, 4 * cr), F32),
            pltpu.VMEM((2 * nq, 2 * cr, 128), jnp.int32),
            pltpu.VMEM((2 * nq, 8, 4 * cr), jnp.int32),
            dma((nq + 1,)),
            dma((2, nq)), dma((2, nq)), dma((2, nq)), dma((2, nq)),
            dma((2, nq)), dma((2, nq)), dma((2, nq)), dma((2, nq)),
            dma((2, nq)), dma((2,)), dma((n,)), dma((n,)), dma((n,)), dma((n,)),
        ],
        compiler_params=pltpu.CompilerParams(
            collective_id=0, has_side_effects=True, vmem_limit_bytes=48 * 2**20
        ),
    )(packed.reshape(nq + 1, 2 * cr, width), idm, key)
    return out.reshape(rows)


def solution(mesh):
    n = mesh.shape["blk"] * mesh.shape["split"]
    spec = P(("groups", "blk", "split"))
    return jax.shard_map(
        functools.partial(body, n),
        mesh=mesh,
        in_specs=(P(("groups", "blk", "split"), None), spec, spec),
        out_specs=spec,
        check_vma=False,
    )
```
